32 devices in a mesh: gx: 8 (over z, x), gy: 4 (over y, core).
Axes of the slice: x: 2, y: 2, z: 4, core: 2. Of those that a mesh axis runs over, the one named last changes fastest.
Arguments:
- fine_cotangent: float32 [2, 128, 1024], P(None, 'gx', 'gy'), may hold values from -6 to 6
- coarse_cotangent: float32 [2, 128, 1024], P(None, 'gx', 'gy'), may hold values from -6 to 6
- upstream_x: int32 [3, 8], replicated, may hold values from -16 to 16, as said below
- upstream_y: int32 [3, 1], replicated, may hold values from -32 to 32, as said below
- fractions: float32 [3, 2], replicated, may hold values from 0.05 to 0.95
Outputs:
- difference: float32 [2, 128, 1024], P(None, 'gx', 'gy')
The draws below stay inside these ranges and needn't reach their ends.
Inputs may be any that keep to these rules, and one draw needn't show every extreme that they name: `upstream_x`: each entry lies in -16 to 16; both ends occur in every draw. `upstream_y`: each entry lies in -32 to 32; both ends occur in every draw.
All inputs are finite; a program needn't handle non-finite values.
Results may differ from the reference program's by a relative error of at most 0.00002.
Values sent between devices are 32-bit elements; how exact they have to be, the bound alone decides.
No kernel may reach another device: no remote copies, remote signals or barrier semaphores. Data moves between devices by JAX's collectives and lax.ppermute only.
A program may use at most 64 MiB of HBM per device.

```python
import jax
import jax.numpy as jnp

NZ = 2
LINE = 128
MAXDY = 32
MAXD = 16
NX = 128
NY = 1024


def reach_both(key, total_count, largest):
    first_key, second_key = jax.random.split(key)
    values = jax.random.randint(first_key, (total_count,), -largest, largest + 1)
    ranking = jax.random.permutation(second_key, total_count)
    positions = jnp.arange(total_count)
    values = jnp.where(positions == ranking[0], largest, values)
    values = jnp.where(positions == ranking[1], -largest, values)
    return values.astype(jnp.int32)


def draw_upstream_x(key, part):
    return reach_both(jax.random.fold_in(key, 11), 3 * (NY // LINE), MAXD).reshape(3, NY // LINE)


def draw_upstream_y(key, part):
    return reach_both(jax.random.fold_in(key, 23), 3 * (NX // LINE), MAXDY).reshape(3, NX // LINE)


def level_of(key, dims, cuts, least, high):
    def one(dim, blocks):
        heights = jax.random.uniform(jax.random.fold_in(jax.random.fold_in(key, 6), dim), (blocks,), jnp.float32, least / len(cuts), high / len(cuts))
        return jnp.repeat(jnp.exp(heights), dims[dim] // blocks).reshape((-1,) + (1,) * (len(dims) - dim - 1))

    loudness = one(*cuts[0])
    for cut in cuts[1:]:
        loudness = loudness * one(*cut)
    return loudness


def normal_values(key, dims, deviation, reach, shards=(), held_as=jnp.bfloat16):
    factor_of = level_of(key, dims, shards, -0.22, 0.18) if shards else 1.0
    drawn = jax.random.normal(key, dims, jnp.float32) * deviation * factor_of
    return jnp.minimum(jnp.maximum(drawn, -reach), reach).astype(held_as)


def setup_inputs(seed: int = 0) -> dict:
    seeds = jax.random.split(jax.random.key(seed), 6)
    return {
        "fine_cotangent": normal_values(seeds[0], (NZ, NX, NY), 1.0, 6.0, ((1, 8), (2, 4)), jnp.float32),
        "coarse_cotangent": normal_values(seeds[1], (NZ, NX, NY), 1.0, 6.0, ((1, 8), (2, 4)), jnp.float32),
        "upstream_x": draw_upstream_x(jax.random.fold_in(seeds[5], 71), 0),
        "upstream_y": draw_upstream_y(jax.random.fold_in(seeds[5], 71), 0),
        "fractions": jnp.clip(jax.random.uniform(seeds[4], (3, 2), jnp.float32, 0.05, 0.95), 0.05, 0.95),
    }


def cubic_weights(fraction):
    position = 1.0 - fraction
    return (-position * (position - 1.0) * (position - 2.0) / 6.0,
            (position + 1.0) * (position - 1.0) * (position - 2.0) / 2.0,
            -(position + 1.0) * position * (position - 2.0) / 2.0,
            (position + 1.0) * position * (position - 1.0) / 6.0)


def sweep_axis(incoming, shifts, weights, block_axis, roll_axis, block_total):
    pieces = []
    for block_index in range(block_total):
        column = jax.lax.slice_in_dim(incoming, block_index * LINE, (block_index + 1) * LINE, axis=block_axis)
        summed = weights[0] * jnp.roll(column, -(shifts[block_index] + 2), axis=roll_axis)
        for tap_index in range(1, 4):
            summed = summed + weights[tap_index] * jnp.roll(column, -(shifts[block_index] + 2 - tap_index), axis=roll_axis)
        pieces.append(summed)
    return jnp.concatenate(pieces, axis=block_axis)


def adjoint_pass(incoming, upstream_x, upstream_y, fractions, pass_row):
    along_x = cubic_weights(fractions[pass_row, 0])
    along_y = cubic_weights(fractions[pass_row, 1])
    swept = sweep_axis(incoming, upstream_x[pass_row], along_x, 2, 1, NY // LINE)
    return sweep_axis(swept, upstream_y[pass_row], along_y, 1, 2, NX // LINE)


def reference(fine_cotangent, coarse_cotangent, upstream_x, upstream_y, fractions):
    fine_field = adjoint_pass(fine_cotangent, upstream_x, upstream_y, fractions, 1)
    fine_field = adjoint_pass(fine_field, upstream_x, upstream_y, fractions, 0)
    coarse_field = adjoint_pass(coarse_cotangent, upstream_x, upstream_y, fractions, 2)
    return fine_field - coarse_field
```

```python
import functools

import jax
import jax.numpy as jnp
from jax import lax
from jax.experimental import pallas as pl
from jax.experimental.pallas import tpu as pltpu
from jax.sharding import PartitionSpec as P

LINE = 128
MAXDY = 32
EDGE = 8


def rounded(rows):
    return -(-rows // EDGE) * EDGE


def shifted(block, axis, distance):
    count = lax.axis_size(axis)
    return lax.ppermute(block, axis, [((i - distance) % count, i) for i in range(count)])


def ring_window(block, slabs):
    lower = [shifted(block, "gx", distance) for distance in range(slabs, 0, -1)]
    upper = [shifted(block, "gx", -distance) for distance in range(1, slabs + 1)]
    return jnp.concatenate(lower + [block] + upper, axis=1)


def cubic_weights(fraction):
    position = 1.0 - fraction
    return (
        -position * (position - 1.0) * (position - 2.0) * (1.0 / 6.0),
        (position + 1.0) * (position - 1.0) * (position - 2.0) * 0.5,
        -(position + 1.0) * position * (position - 2.0) * 0.5,
        (position + 1.0) * position * (position - 1.0) * (1.0 / 6.0),
    )


def weighted(weights, term):
    summed = weights[0] * term(0)
    for tap in range(1, 4):
        summed = summed + weights[tap] * term(tap)
    return summed


def sweep_x_kernel(slab, center_fine, center_coarse,
                   shifts, fractions, fine, coarse, own, own_coarse, to_left, to_right,
                   fine_lines, coarse_lines):
    levels = fine.shape[0]
    lines = own.shape[0]
    rows = own.shape[3]
    total = shifts.shape[1]
    first = lax.axis_index("gy") * lines
    fine_weights = cubic_weights(fractions[1, 0])
    coarse_weights = cubic_weights(fractions[2, 0])
    for line in range(lines):
        lanes = slice(line * LINE, (line + 1) * LINE)
        fine_lines[line] = fine[:, :, lanes]
        coarse_lines[line] = coarse[:, :, lanes]
        inner = shifts[1, first + line]
        for slot in range(3):
            region = lax.rem(first + line + slot - 1 + total, total)
            start = center_fine - 1 + inner + shifts[0, region]
            for level in range(levels):
                summed = weighted(
                    fine_weights,
                    lambda tap: fine_lines[line, level, pl.ds(start + 2 - tap, rows)],
                )
                own[line, slot, level] = summed
                if line == 0 and slot < 2:
                    to_left[level, slot * rows:(slot + 1) * rows] = summed
                if line == lines - 1 and slot > 0:
                    to_right[level, (slot - 1) * rows:slot * rows] = summed
        start = center_coarse + shifts[2, first + line]
        for level in range(levels):
            summed = weighted(
                coarse_weights,
                lambda tap: coarse_lines[line, level, pl.ds(start + 2 - tap, slab)],
            )
            own_coarse[line, level] = summed
            if line == 0:
                to_left[level, 2 * rows:] = summed
            if line == lines - 1:
                to_right[level, 2 * rows:] = summed


def turned(weights, offset, current, left, right, lane):
    beside = jnp.where(lane < LINE // 2, right, left)

    def term(tap):
        distance = offset + 2 - tap
        outside = (lane < distance) | (lane >= LINE + distance)
        mixed = jnp.where(outside, beside, current)
        return pltpu.roll(mixed, lax.rem(LINE - distance, LINE), 1)

    return weighted(weights, term)


def sweep_y_kernel(shifts_x, shifts_y, fractions, own, own_coarse, from_left, from_right,
                   out, held):
    lines, _, levels, rows, _ = own.shape
    slab = own_coarse.shape[2]
    total = shifts_x.shape[1]
    strips = shifts_y.shape[1]
    first = lax.axis_index("gy") * lines
    base = lax.axis_index("gx") * slab
    extent = lax.axis_size("gx") * slab
    outer_x = cubic_weights(fractions[0, 0])
    outer_y = cubic_weights(fractions[0, 1])
    inner_y = cubic_weights(fractions[1, 1])
    coarse_y = cubic_weights(fractions[2, 1])
    tall = lax.broadcasted_iota(jnp.int32, (rows, LINE), 1)
    flat = lax.broadcasted_iota(jnp.int32, (slab, LINE), 1)
    strip = lax.div(base, LINE)

    def pieces(region, level):
        if region < 0:
            current = from_left[level, 0:rows]
            return current, current, own[0, 0, level]
        if region == lines:
            current = from_right[level, rows:2 * rows]
            return current, own[lines - 1, 2, level], current
        left = own[region - 1, 2, level] if region else from_left[level, rows:2 * rows]
        right = own[region + 1, 0, level] if region < lines - 1 else from_right[level, 0:rows]
        return own[region, 1, level], left, right

    outer = {}
    for region in range(-1, lines + 1):
        if strips > 1:
            shift = shifts_x[0, lax.rem(first + region + total, total)]
            start = lax.rem(base + shift - 1 + extent, extent)
            here = lax.div(start, LINE)
            after = lax.rem(here + 1, strips)
            row = lax.broadcasted_iota(jnp.int32, (rows, LINE), 0)
            beyond = row >= LINE - lax.rem(start, LINE)
        for level in range(levels):
            current, left, right = pieces(region, level)
            if strips > 1:
                swept = jnp.where(
                    beyond,
                    turned(inner_y, shifts_y[1, after], current, left, right, tall),
                    turned(inner_y, shifts_y[1, here], current, left, right, tall),
                )
            else:
                swept = turned(inner_y, shifts_y[1, 0], current, left, right, tall)
            held[region + 1, level] = swept
            outer[region, level] = weighted(
                outer_x, lambda tap: held[region + 1, level, 3 - tap:3 - tap + slab]
            )
    for line in range(lines):
        for level in range(levels):
            fine_field = turned(
                outer_y, shifts_y[0, strip], outer[line, level],
                outer[line - 1, level], outer[line + 1, level], flat,
            )
            left = own_coarse[line - 1, level] if line else from_left[level, 2 * rows:]
            right = own_coarse[line + 1, level] if line < lines - 1 else from_right[level, 2 * rows:]
            coarse_field = turned(
                coarse_y, shifts_y[2, strip], own_coarse[line, level], left, right, flat
            )
            out[level, :, line * LINE:(line + 1) * LINE] = fine_field - coarse_field


def on_chip(count):
    return [pl.BlockSpec(memory_space=pltpu.VMEM)] * count


def scalars(count):
    return [pl.BlockSpec(memory_space=pltpu.SMEM)] * count


def local(fine_cotangent, coarse_cotangent, upstream_x, upstream_y, fractions):
    levels, slab, width = fine_cotangent.shape
    lines = width // LINE
    reach = lax.axis_size("gx") // 8 * slab
    rows = rounded(slab + 3)
    slabs_fine = -(-(2 * reach + 4) // slab)
    slabs_coarse = -(-(reach + 2) // slab)
    fine = ring_window(fine_cotangent, slabs_fine)
    coarse = ring_window(coarse_cotangent, slabs_coarse)
    like = functools.partial(jax.ShapeDtypeStruct, dtype=fine.dtype)
    sent = like((levels, 2 * rows + slab, LINE))
    own, own_coarse, to_left, to_right = pl.pallas_call(
        functools.partial(sweep_x_kernel, slab, slabs_fine * slab, slabs_coarse * slab),
        out_shape=[
            like((lines, 3, levels, rows, LINE)), like((lines, levels, slab, LINE)), sent, sent,
        ],
        in_specs=scalars(2) + on_chip(2),
        out_specs=on_chip(4),
        scratch_shapes=[
            pltpu.VMEM((lines, *block.shape[:2], LINE), fine.dtype) for block in (fine, coarse)
        ],
    )(upstream_x, fractions, fine, coarse)
    from_left = shifted(to_right, "gy", 1)
    from_right = shifted(to_left, "gy", -1)
    return pl.pallas_call(
        sweep_y_kernel,
        out_shape=like((levels, slab, width)),
        in_specs=scalars(3) + on_chip(4),
        out_specs=on_chip(1)[0],
        scratch_shapes=[pltpu.VMEM((lines + 2, levels, rows, LINE), fine.dtype)],
    )(upstream_x, upstream_y, fractions, own, own_coarse, from_left, from_right)


def solution(mesh):
    placed = (P(None, "gx", "gy"), P(None, "gx", "gy"), P(), P(), P())
    return jax.shard_map(
        local, mesh=mesh, in_specs=placed, out_specs=P(None, "gx", "gy"), check_vma=False
    )
```

```python
import functools

import jax
import jax.numpy as jnp
from jax import lax
from jax.experimental import pallas as pl
from jax.experimental.pallas import tpu as pltpu
from jax.sharding import PartitionSpec as P

LINE = 128
MAXDY = 32
EDGE = 8


def rounded(rows):
    return -(-rows // EDGE) * EDGE


def exchanged(block, axis, partner):
    return lax.ppermute(block, axis, [(i, partner(i)) for i in range(lax.axis_size(axis))])


def shifted(block, axis, distance):
    count = lax.axis_size(axis)
    return exchanged(block, axis, lambda i: (i + distance) % count)


def ring_window(block, slabs):
    lower = [shifted(block, "gx", distance) for distance in range(slabs, 0, -1)]
    upper = [shifted(block, "gx", -distance) for distance in range(1, slabs + 1)]
    return jnp.concatenate(lower + [block] + upper, axis=1)


def cubic_weights(fraction):
    position = 1.0 - fraction
    return (
        -position * (position - 1.0) * (position - 2.0) * (1.0 / 6.0),
        (position + 1.0) * (position - 1.0) * (position - 2.0) * 0.5,
        -(position + 1.0) * position * (position - 2.0) * 0.5,
        (position + 1.0) * position * (position - 1.0) * (1.0 / 6.0),
    )


def weighted(weights, term):
    summed = weights[0] * term(0)
    for tap in range(1, 4):
        summed = summed + weights[tap] * term(tap)
    return summed


def aligned(start, size):
    return pl.ds(pl.multiple_of(start, EDGE), size)


def column_side():
    return lax.axis_index("gx") % 2


def layer_side():
    return lax.axis_index("gx") // 2 % 2


def relay_kernel(near, far, opposite, relay):
    both = near.shape[1]
    slab = both // 2
    column = column_side()
    start = (1 - column) * (slab - EDGE)
    swapped = (column + layer_side()) % 2

    def send(whole, partial):
        relay[:, :both] = whole[...]
        relay[:, both:both + EDGE] = partial[:, aligned(start, EDGE)]

    @pl.when(swapped == 0)
    def _():
        send(near, far)

    @pl.when(swapped == 1)
    def _():
        send(far, near)

    relay[:, both + EDGE:] = opposite[...]


def fill_whole(fine, coarse, fine_lines, coarse_lines):
    for line in range(fine_lines.shape[0]):
        lanes = slice(line * LINE, (line + 1) * LINE)
        fine_lines[line] = fine[:, :, lanes]
        coarse_lines[line] = coarse[:, :, lanes]


def fill_pieces(own, beside, near, far, relay, fine_lines, coarse_lines):
    both = own.shape[1]
    slab = both // 2
    column = 1 - 2 * column_side()
    layer = 1 - 2 * layer_side()
    fine_center = (fine_lines.shape[2] - slab) // 2
    coarse_center = (coarse_lines.shape[2] - slab) // 2
    below = fine_center - 2 * slab - EDGE
    above = fine_center + 3 * slab
    for line in range(fine_lines.shape[0]):
        lanes = slice(line * LINE, (line + 1) * LINE)
        for piece, slabs in (
            (own, 0), (beside, column), (near, 2 * layer), (far, -2 * layer), (relay, -column),
        ):
            fine_lines[line, :, aligned(fine_center + slabs * slab, slab)] = piece[:, :slab, lanes]
            coarse_lines[line, :, aligned(coarse_center + slabs * slab, slab)] = (
                piece[:, slab:both, lanes]
            )
        for start, up in ((both, column), (both + EDGE, -column)):
            row = below + (above - below) // 2 * (1 + up)
            fine_lines[line, :, aligned(row, EDGE)] = relay[:, start:start + EDGE, lanes]


def sweep_x_kernel(fill, shifts, fractions, *refs):
    *gathered, own, own_coarse, to_near, to_far, fine_lines, coarse_lines = refs
    lines, levels, _, _ = fine_lines.shape
    rows = own.shape[3]
    slab = own_coarse.shape[2]
    total = shifts.shape[1]
    first = lax.axis_index("gy") * lines
    fine_center = (fine_lines.shape[2] - slab) // 2
    coarse_center = (coarse_lines.shape[2] - slab) // 2
    fine_weights = cubic_weights(fractions[0, 1])
    coarse_weights = cubic_weights(fractions[0, 2])
    fill(*gathered, fine_lines, coarse_lines)
    for line in range(lines):
        inner = shifts[1, first + line]
        for slot in range(3):
            region = lax.rem(first + line + slot - 1 + total, total)
            start = fine_center - 1 + inner + shifts[0, region]
            for level in range(levels):
                own[line, slot, level] = weighted(
                    fine_weights,
                    lambda tap: fine_lines[line, level, pl.ds(start + 2 - tap, rows)],
                )
        start = coarse_center + shifts[2, first + line]
        for level in range(levels):
            own_coarse[line, level] = weighted(
                coarse_weights,
                lambda tap: coarse_lines[line, level, pl.ds(start + 2 - tap, slab)],
            )
    near_right = lax.axis_index("gy") % 2 == 0
    for level in range(levels):
        leftward = own[0, 0, level], own[0, 1, level], own_coarse[0, level]
        rightward = own[lines - 1, 1, level], own[lines - 1, 2, level], own_coarse[lines - 1, level]
        for start, left, right in zip((0, rows, 2 * rows), leftward, rightward):
            part = slice(start, start + left.shape[0])
            to_near[level, part] = jnp.where(near_right, right, left)
            to_far[level, part] = jnp.where(near_right, left, right)


def turned(weights, offset, current, left, right, lane):
    beside = jnp.where(lane < LINE // 2, right, left)

    def term(tap):
        distance = offset + 2 - tap
        outside = (lane < distance) | (lane >= LINE + distance)
        mixed = jnp.where(outside, beside, current)
        return pltpu.roll(mixed, lax.rem(LINE - distance, LINE), 1)

    return weighted(weights, term)


def sweep_y_kernel(shifts_x, shifts_y, fractions, own, own_coarse, from_near, from_far, out, held):
    lines, _, levels, rows, _ = own.shape
    slab = own_coarse.shape[2]
    total = shifts_x.shape[1]
    strips = shifts_y.shape[0]
    first = lax.axis_index("gy") * lines
    base = lax.axis_index("gx") * slab
    extent = lax.axis_size("gx") * slab
    outer_x = cubic_weights(fractions[0, 0])
    outer_y = cubic_weights(fractions[1, 0])
    inner_y = cubic_weights(fractions[1, 1])
    coarse_y = cubic_weights(fractions[1, 2])
    tall = lax.broadcasted_iota(jnp.int32, (rows, LINE), 1)
    flat = lax.broadcasted_iota(jnp.int32, (slab, LINE), 1)
    strip = lax.div(base, LINE)
    near_right = lax.axis_index("gy") % 2 == 0

    def from_left(level, start, size):
        part = slice(start, start + size)
        return jnp.where(near_right, from_far[level, part], from_near[level, part])

    def from_right(level, start, size):
        part = slice(start, start + size)
        return jnp.where(near_right, from_near[level, part], from_far[level, part])

    def pieces(region, level):
        if region < 0:
            current = from_left(level, 0, rows)
            return current, current, own[0, 0, level]
        if region == lines:
            current = from_right(level, rows, rows)
            return current, own[lines - 1, 2, level], current
        left = own[region - 1, 2, level] if region else from_left(level, rows, rows)
        right = own[region + 1, 0, level] if region < lines - 1 else from_right(level, 0, rows)
        return own[region, 1, level], left, right

    outer = {}
    for region in range(-1, lines + 1):
        if strips > 1:
            shift = shifts_x[0, lax.rem(first + region + total, total)]
            start = lax.rem(base + shift - 1 + extent, extent)
            here = lax.div(start, LINE)
            after = lax.rem(here + 1, strips)
            row = lax.broadcasted_iota(jnp.int32, (rows, LINE), 0)
            beyond = row >= LINE - lax.rem(start, LINE)
        for level in range(levels):
            current, left, right = pieces(region, level)
            if strips > 1:
                swept = jnp.where(
                    beyond,
                    turned(inner_y, shifts_y[after, 1], current, left, right, tall),
                    turned(inner_y, shifts_y[here, 1], current, left, right, tall),
                )
            else:
                swept = turned(inner_y, shifts_y[0, 1], current, left, right, tall)
            held[region + 1, level] = swept
            outer[region, level] = weighted(
                outer_x, lambda tap: held[region + 1, level, 3 - tap:3 - tap + slab]
            )
    for line in range(lines):
        for level in range(levels):
            fine_field = turned(
                outer_y, shifts_y[strip, 0], outer[line, level],
                outer[line - 1, level], outer[line + 1, level], flat,
            )
            left = own_coarse[line - 1, level] if line else from_left(level, 2 * rows, slab)
            right = (
                own_coarse[line + 1, level] if line < lines - 1
                else from_right(level, 2 * rows, slab)
            )
            coarse_field = turned(
                coarse_y, shifts_y[strip, 2], own_coarse[line, level], left, right, flat
            )
            out[level, :, line * LINE:(line + 1) * LINE] = fine_field - coarse_field


def on_chip(count):
    return [pl.BlockSpec(memory_space=pltpu.VMEM)] * count


def scalars(count):
    return [pl.BlockSpec(memory_space=pltpu.SMEM)] * count


def local(fine_cotangent, coarse_cotangent, upstream_x, upstream_y, fractions):
    levels, slab, width = fine_cotangent.shape
    lines = width // LINE
    count_x = lax.axis_size("gx")
    count_y = lax.axis_size("gy")
    reach = count_x // 8 * slab
    rows = rounded(slab + 3)
    slabs_fine = -(-(2 * reach + 4) // slab)
    slabs_coarse = -(-(reach + 2) // slab)
    like = functools.partial(jax.ShapeDtypeStruct, dtype=fine_cotangent.dtype)
    windows = [
        pltpu.VMEM((lines, levels, (2 * slabs + 1) * slab, LINE), fine_cotangent.dtype)
        for slabs in (slabs_fine, slabs_coarse)
    ]
    limit = (4 << 20) + 12 * levels * (slabs_fine + slabs_coarse + 1) * slab * width * 4
    params = pltpu.CompilerParams(vmem_limit_bytes=limit)
    if count_x == 8 and slab == 2 * EDGE:
        packed = jnp.concatenate([fine_cotangent, coarse_cotangent], axis=1)
        packed = lax.optimization_barrier(packed)
        edge = lax.dynamic_slice_in_dim(packed, column_side() * (slab - EDGE), EDGE, 1)
        beside = exchanged(packed, "gx", lambda i: i ^ 1)
        near = exchanged(packed, "gx", lambda i: i ^ 2)
        opposite = exchanged(edge, "gx", lambda i: i ^ 4)
        far = exchanged(packed, "gx", lambda i: i ^ 6)
        beside, near, opposite, far = lax.optimization_barrier((beside, near, opposite, far))
        relay = pl.pallas_call(
            relay_kernel,
            out_shape=like((levels, 2 * slab + 2 * EDGE, width)),
            in_specs=on_chip(3),
            out_specs=on_chip(1)[0],
            compiler_params=params,
        )(near, far, opposite)
        relay = exchanged(relay, "gx", lambda i: i ^ 1)
        fill = fill_pieces
        gathered = packed, beside, near, far, relay
    else:
        fill = fill_whole
        gathered = ring_window(fine_cotangent, slabs_fine), ring_window(coarse_cotangent, slabs_coarse)
    sent = like((levels, 2 * rows + slab, LINE))
    own, own_coarse, to_near, to_far = pl.pallas_call(
        functools.partial(sweep_x_kernel, fill),
        out_shape=[
            like((lines, 3, levels, rows, LINE)), like((lines, levels, slab, LINE)), sent, sent,
        ],
        in_specs=scalars(2) + on_chip(len(gathered)),
        out_specs=on_chip(4),
        scratch_shapes=windows,
        compiler_params=params,
    )(upstream_x, fractions.T, *gathered)
    from_near = exchanged(to_near, "gy", lambda j: j ^ 1)
    from_far = exchanged(to_far, "gy", lambda j: (j - 1 + 2 * (j % 2)) % count_y)
    return pl.pallas_call(
        sweep_y_kernel,
        out_shape=like((levels, slab, width)),
        in_specs=scalars(3) + on_chip(4),
        out_specs=on_chip(1)[0],
        scratch_shapes=[pltpu.VMEM((lines + 2, levels, rows, LINE), fine_cotangent.dtype)],
        compiler_params=params,
    )(upstream_x, upstream_y.T, fractions.T, own, own_coarse, from_near, from_far)


def solution(mesh):
    placed = (P(None, "gx", "gy"), P(None, "gx", "gy"), P(), P(), P())
    return jax.shard_map(
        local, mesh=mesh, in_specs=placed, out_specs=P(None, "gx", "gy"), check_vma=False
    )
```

```python
import functools

import jax
import jax.numpy as jnp
from jax import lax
from jax.experimental import pallas as pl
from jax.experimental.pallas import tpu as pltpu
from jax.sharding import PartitionSpec as P


LINE = 128
MAXDY = 32
EDGE = 8
HALO = MAXDY + 2


def rounded(rows):
    return -(-rows // EDGE) * EDGE


def exchanged(block, axis, partner):
    return lax.ppermute(block, axis, [(i, partner(i)) for i in range(lax.axis_size(axis))])


def shifted(block, axis, distance):
    count = lax.axis_size(axis)
    return exchanged(block, axis, lambda i: (i + distance) % count)


def ring_window(block, slabs):
    lower = [shifted(block, "gx", distance) for distance in range(slabs, 0, -1)]
    upper = [shifted(block, "gx", -distance) for distance in range(1, slabs + 1)]
    return jnp.concatenate(lower + [block] + upper, axis=1)


def cubic_weights(fraction):
    position = 1.0 - fraction
    return (
        -position * (position - 1.0) * (position - 2.0) * (1.0 / 6.0),
        (position + 1.0) * (position - 1.0) * (position - 2.0) * 0.5,
        -(position + 1.0) * position * (position - 2.0) * 0.5,
        (position + 1.0) * position * (position - 1.0) * (1.0 / 6.0),
    )


def weighted(weights, term):
    summed = weights[0] * term(0)
    for tap in range(1, 4):
        summed = summed + weights[tap] * term(tap)
    return summed


def aligned(start, size):
    return pl.ds(pl.multiple_of(start, EDGE), size)


def column_side():
    return lax.axis_index("gx") % 2


def layer_side():
    return lax.axis_index("gx") // 2 % 2


def relay_kernel(near, far, opposite, relay):
    levels, both, width = near.shape
    slab = both // 2
    column = column_side()
    start = (1 - column) * (slab - EDGE)
    swapped = (column + layer_side()) % 2
    row = lax.broadcasted_iota(jnp.int32, (levels, EDGE, width), 1)
    low = (row < EDGE // 2) == (column == 1)

    def send(whole, partial):
        relay[:, :both] = whole[...]
        relay[:, both:] = jnp.where(low, partial[:, aligned(start, EDGE)], opposite[...])

    @pl.when(swapped == 0)
    def _():
        send(near, far)

    @pl.when(swapped == 1)
    def _():
        send(far, near)


def fill_whole(fine, coarse, fine_lines, coarse_lines):
    for line in range(fine_lines.shape[0]):
        lanes = slice(line * LINE, (line + 1) * LINE)
        fine_lines[line] = fine[:, :, lanes]
        coarse_lines[line] = coarse[:, :, lanes]


def fill_pieces(own, beside, near, far, relay, fine_lines, coarse_lines):
    both = own.shape[1]
    slab = both // 2
    column = 1 - 2 * column_side()
    layer = 1 - 2 * layer_side()
    fine_center = (fine_lines.shape[2] - slab) // 2
    coarse_center = (coarse_lines.shape[2] - slab) // 2
    below = fine_center - 2 * slab - EDGE
    above = fine_center + 3 * slab
    for line in range(fine_lines.shape[0]):
        lanes = slice(line * LINE, (line + 1) * LINE)
        for piece, slabs in (
            (own, 0), (beside, column), (near, 2 * layer), (far, -2 * layer), (relay, -column),
        ):
            fine_lines[line, :, aligned(fine_center + slabs * slab, slab)] = piece[:, :slab, lanes]
            coarse_lines[line, :, aligned(coarse_center + slabs * slab, slab)] = (
                piece[:, slab:both, lanes]
            )
        for row in (below, above):
            fine_lines[line, :, row:row + EDGE] = relay[:, both:, lanes]


def sweep_x_kernel(fill, shifts, _, fractions, *refs):
    *gathered, own, own_coarse, to_near, to_far, fine_lines, coarse_lines = refs
    lines, levels, _, _ = fine_lines.shape
    rows = own.shape[3]
    slab = own_coarse.shape[2]
    total = shifts.shape[1]
    first = lax.axis_index("gy") * lines
    fine_center = (fine_lines.shape[2] - slab) // 2
    coarse_center = (coarse_lines.shape[2] - slab) // 2
    fine_weights = cubic_weights(fractions[0, 1])
    coarse_weights = cubic_weights(fractions[0, 2])
    fill(*gathered, fine_lines, coarse_lines)
    for line in range(lines):
        inner = shifts[1, first + line]
        for slot in range(3):
            region = lax.rem(first + line + slot - 1 + total, total)
            start = fine_center - 1 + inner + shifts[0, region]
            for level in range(levels):
                own[line, slot, level] = weighted(
                    fine_weights,
                    lambda tap: fine_lines[line, level, pl.ds(start + 2 - tap, rows)],
                )
        start = coarse_center + shifts[2, first + line]
        for level in range(levels):
            own_coarse[line, level] = weighted(
                coarse_weights,
                lambda tap: coarse_lines[line, level, pl.ds(start + 2 - tap, slab)],
            )
    near_right = lax.axis_index("gy") % 2 == 0
    half = LINE // 2
    lane = lax.broadcasted_iota(jnp.int32, (rows, LINE), 1)
    flat = lax.broadcasted_iota(jnp.int32, (slab // 2, LINE), 1)
    for level in range(levels):
        last = lines - 1
        left = jnp.where(
            lane < LINE - HALO, own[0, 1, level], pltpu.roll(own[0, 0, level], LINE - HALO, 1)
        )
        right = jnp.where(
            lane >= HALO, own[last, 1, level], pltpu.roll(own[last, 2, level], HALO, 1)
        )
        to_near[level, :rows] = jnp.where(near_right, right, left)
        to_far[level, :rows] = jnp.where(near_right, left, right)
        upper, lower = own_coarse[0, level, :slab // 2], own_coarse[0, level, slab // 2:]
        left = jnp.where(flat < half, upper, pltpu.roll(lower, half, 1))
        upper, lower = own_coarse[last, level, :slab // 2], own_coarse[last, level, slab // 2:]
        right = jnp.where(flat < half, pltpu.roll(upper, half, 1), lower)
        to_near[level, rows:] = jnp.where(near_right, right, left)
        to_far[level, rows:] = jnp.where(near_right, left, right)


def turned(weights, offset, current, left, right, lane):
    beside = jnp.where(lane < LINE // 2, right, left)

    def term(tap):
        distance = offset + 2 - tap
        outside = (lane < distance) | (lane >= LINE + distance)
        mixed = jnp.where(outside, beside, current)
        return pltpu.roll(mixed, lax.rem(LINE - distance, LINE), 1)

    return weighted(weights, term)


def sweep_y_kernel(shifts_x, shifts_y, fractions, own, own_coarse, from_near, from_far, out, held):
    lines, _, levels, rows, _ = own.shape
    slab = own_coarse.shape[2]
    total = shifts_x.shape[1]
    strips = shifts_y.shape[0]
    first = lax.axis_index("gy") * lines
    base = lax.axis_index("gx") * slab
    extent = lax.axis_size("gx") * slab
    outer_x = cubic_weights(fractions[0, 0])
    outer_y = cubic_weights(fractions[1, 0])
    inner_y = cubic_weights(fractions[1, 1])
    coarse_y = cubic_weights(fractions[1, 2])
    tall = lax.broadcasted_iota(jnp.int32, (rows, LINE), 1)
    flat = lax.broadcasted_iota(jnp.int32, (slab, LINE), 1)
    strip = lax.div(base, LINE)
    near_right = lax.axis_index("gy") % 2 == 0

    def received(level):
        near, far = from_near[level], from_far[level]
        left, right = jnp.where(near_right, far, near), jnp.where(near_right, near, far)
        half = LINE // 2
        return {
            "left": (left[:rows], pltpu.roll(left[:rows], LINE - HALO, 1)),
            "right": (right[:rows], pltpu.roll(right[:rows], HALO, 1)),
            "left_coarse": jnp.concatenate([pltpu.roll(left[rows:], half, 1), left[rows:]]),
            "right_coarse": jnp.concatenate([right[rows:], pltpu.roll(right[rows:], half, 1)]),
        }

    halo = [received(level) for level in range(levels)]

    def pieces(region, level):
        if region < 0:
            current = halo[level]["left"][0]
            return current, current, own[0, 0, level]
        if region == lines:
            current = halo[level]["right"][0]
            return current, own[lines - 1, 2, level], current
        left = own[region - 1, 2, level] if region else halo[level]["left"][1]
        right = own[region + 1, 0, level] if region < lines - 1 else halo[level]["right"][1]
        return own[region, 1, level], left, right

    outer = {}
    for region in range(-1, lines + 1):
        if strips > 1:
            shift = shifts_x[0, lax.rem(first + region + total, total)]
            start = lax.rem(base + shift - 1 + extent, extent)
            here = lax.div(start, LINE)
            after = lax.rem(here + 1, strips)
            row = lax.broadcasted_iota(jnp.int32, (rows, LINE), 0)
            beyond = row >= LINE - lax.rem(start, LINE)
        for level in range(levels):
            current, left, right = pieces(region, level)
            if strips > 1:
                swept = jnp.where(
                    beyond,
                    turned(inner_y, shifts_y[after, 1], current, left, right, tall),
                    turned(inner_y, shifts_y[here, 1], current, left, right, tall),
                )
            else:
                swept = turned(inner_y, shifts_y[0, 1], current, left, right, tall)
            held[region + 1, level] = swept
            outer[region, level] = weighted(
                outer_x, lambda tap: held[region + 1, level, 3 - tap:3 - tap + slab]
            )
    for line in range(lines):
        for level in range(levels):
            fine_field = turned(
                outer_y, shifts_y[strip, 0], outer[line, level],
                outer[line - 1, level], outer[line + 1, level], flat,
            )
            left = own_coarse[line - 1, level] if line else halo[level]["left_coarse"]
            right = (
                own_coarse[line + 1, level] if line < lines - 1 else halo[level]["right_coarse"]
            )
            coarse_field = turned(
                coarse_y, shifts_y[strip, 2], own_coarse[line, level], left, right, flat
            )
            out[level, :, line * LINE:(line + 1) * LINE] = fine_field - coarse_field


def on_chip(count):
    return [pl.BlockSpec(memory_space=pltpu.VMEM)] * count


def scalars(count):
    return [pl.BlockSpec(memory_space=pltpu.SMEM)] * count


def local(fine_cotangent, coarse_cotangent, upstream_x, upstream_y, fractions):
    levels, slab, width = fine_cotangent.shape
    lines = width // LINE
    count_x = lax.axis_size("gx")
    count_y = lax.axis_size("gy")
    reach = count_x // 8 * slab
    rows = rounded(slab + 3)
    slabs_fine = -(-(2 * reach + 4) // slab)
    slabs_coarse = -(-(reach + 2) // slab)
    like = functools.partial(jax.ShapeDtypeStruct, dtype=fine_cotangent.dtype)
    windows = [
        pltpu.VMEM((lines, levels, (2 * slabs + 1) * slab, LINE), fine_cotangent.dtype)
        for slabs in (slabs_fine, slabs_coarse)
    ]
    limit = (4 << 20) + 12 * levels * (slabs_fine + slabs_coarse + 1) * slab * width * 4
    params = pltpu.CompilerParams(vmem_limit_bytes=limit)
    if count_x == 8 and slab == 2 * EDGE:
        packed = jnp.concatenate([fine_cotangent, coarse_cotangent], axis=1)
        packed = lax.optimization_barrier(packed)
        edge = lax.dynamic_slice_in_dim(packed, column_side() * (slab - EDGE), EDGE, 1)
        beside = exchanged(packed, "gx", lambda i: i ^ 1)
        near = exchanged(packed, "gx", lambda i: i ^ 2)
        opposite = exchanged(edge, "gx", lambda i: i ^ 4)
        far = exchanged(packed, "gx", lambda i: i ^ 6)
        beside, near, opposite, far = lax.optimization_barrier((beside, near, opposite, far))
        relay = pl.pallas_call(
            relay_kernel,
            out_shape=like((levels, 2 * slab + EDGE, width)),
            in_specs=on_chip(3),
            out_specs=on_chip(1)[0],
            compiler_params=params,
        )(near, far, opposite)
        relay = exchanged(relay, "gx", lambda i: i ^ 1)
        fill = fill_pieces
        gathered = packed, beside, near, far, relay
    else:
        fill = fill_whole
        gathered = ring_window(fine_cotangent, slabs_fine), ring_window(coarse_cotangent, slabs_coarse)
    sent = like((levels, rows + slab // 2, LINE))
    own, own_coarse, to_near, to_far = pl.pallas_call(
        functools.partial(sweep_x_kernel, fill),
        out_shape=[
            like((lines, 3, levels, rows, LINE)), like((lines, levels, slab, LINE)), sent, sent,
        ],
        in_specs=scalars(3) + on_chip(len(gathered)),
        out_specs=on_chip(4),
        scratch_shapes=windows,
        compiler_params=params,
    )(upstream_x, upstream_y.T, fractions.T, *gathered)
    from_near = exchanged(to_near, "gy", lambda j: j ^ 1)
    from_far = exchanged(to_far, "gy", lambda j: (j - 1 + 2 * (j % 2)) % count_y)
    return pl.pallas_call(
        sweep_y_kernel,
        out_shape=like((levels, slab, width)),
        in_specs=scalars(3) + on_chip(4),
        out_specs=on_chip(1)[0],
        scratch_shapes=[pltpu.VMEM((lines + 2, levels, rows, LINE), fine_cotangent.dtype)],
        compiler_params=params,
    )(upstream_x, upstream_y.T, fractions.T, own, own_coarse, from_near, from_far)


def solution(mesh):
    placed = (P(None, "gx", "gy"), P(None, "gx", "gy"), P(), P(), P())

    def step(*args):
        return local(*args)

    step = jax.shard_map(
        step, mesh=mesh, in_specs=placed, out_specs=P(None, "gx", "gy"), check_vma=False
    )
    return step
```

```python
import functools

import jax
import jax.numpy as jnp
from jax import lax
from jax.experimental import pallas as pl
from jax.experimental.pallas import tpu as pltpu
from jax.sharding import PartitionSpec as P


LINE = 128
MAXDY = 32
EDGE = 8
HALO = MAXDY + 2


def rounded(rows):
    return -(-rows // EDGE) * EDGE


def exchanged(block, axis, partner):
    return lax.ppermute(block, axis, [(i, partner(i)) for i in range(lax.axis_size(axis))])


def shifted(block, axis, distance):
    count = lax.axis_size(axis)
    return exchanged(block, axis, lambda i: (i + distance) % count)


def ring_window(block, slabs):
    lower = [shifted(block, "gx", distance) for distance in range(slabs, 0, -1)]
    upper = [shifted(block, "gx", -distance) for distance in range(1, slabs + 1)]
    return jnp.concatenate(lower + [block] + upper, axis=1)


def cubic_weights(fraction):
    position = 1.0 - fraction
    return (
        -position * (position - 1.0) * (position - 2.0) * (1.0 / 6.0),
        (position + 1.0) * (position - 1.0) * (position - 2.0) * 0.5,
        -(position + 1.0) * position * (position - 2.0) * 0.5,
        (position + 1.0) * position * (position - 1.0) * (1.0 / 6.0),
    )


def weighted(weights, term):
    summed = weights[0] * term(0)
    for tap in range(1, 4):
        summed = summed + weights[tap] * term(tap)
    return summed


def aligned(start, size):
    return pl.ds(pl.multiple_of(start, EDGE), size)


def column_side():
    return lax.axis_index("gx") % 2


def layer_side():
    return lax.axis_index("gx") // 2 % 2


def relay_kernel(near, far, opposite, relay):
    levels, both, width = near.shape
    slab = both // 2
    column = column_side()
    start = (1 - column) * (slab - EDGE)
    swapped = (column + layer_side()) % 2
    row = lax.broadcasted_iota(jnp.int32, (levels, EDGE, width), 1)
    low = (row < EDGE // 2) == (column == 1)

    def send(whole, partial):
        relay[:, :both] = whole[...]
        relay[:, both:] = jnp.where(low, partial[:, aligned(start, EDGE)], opposite[...])

    @pl.when(swapped == 0)
    def _():
        send(near, far)

    @pl.when(swapped == 1)
    def _():
        send(far, near)


def fill_whole(fine, coarse, fine_lines, coarse_lines):
    for line in range(fine_lines.shape[0]):
        lanes = slice(line * LINE, (line + 1) * LINE)
        fine_lines[line] = fine[:, :, lanes]
        coarse_lines[line] = coarse[:, :, lanes]


def fill_pieces(own, beside, near, far, relay, fine_lines, coarse_lines):
    both = own.shape[1]
    slab = both // 2
    column = 1 - 2 * column_side()
    layer = 1 - 2 * layer_side()
    fine_center = (fine_lines.shape[2] - slab) // 2
    coarse_center = (coarse_lines.shape[2] - slab) // 2
    below = fine_center - 2 * slab - EDGE
    above = fine_center + 3 * slab
    for line in range(fine_lines.shape[0]):
        lanes = slice(line * LINE, (line + 1) * LINE)
        for piece, slabs in (
            (own, 0), (beside, column), (near, 2 * layer), (far, -2 * layer), (relay, -column),
        ):
            fine_lines[line, :, aligned(fine_center + slabs * slab, slab)] = piece[:, :slab, lanes]
            coarse_lines[line, :, aligned(coarse_center + slabs * slab, slab)] = (
                piece[:, slab:both, lanes]
            )
        for row in (below, above):
            fine_lines[line, :, row:row + EDGE] = relay[:, both:, lanes]


def table_kernel(slab, lines, fine_center, coarse_center,
                 shifts_x, shifts_y, fractions, offsets, weights):
    total = shifts_x.shape[1]
    strips = shifts_y.shape[0]
    first = lax.axis_index("gy") * lines
    base = lax.axis_index("gx") * slab
    extent = lax.axis_size("gx") * slab
    values = []
    for line in range(lines):
        inner = shifts_x[1, first + line]
        for slot in range(3):
            region = lax.rem(first + line + slot - 1 + total, total)
            values.append(fine_center - 1 + inner + shifts_x[0, region])
        values.append(coarse_center + shifts_x[2, first + line])
    strip = lax.div(base, LINE)
    values += [shifts_y[strip, 0], shifts_y[strip, 2]]
    for region in range(-1, lines + 1):
        shift = shifts_x[0, lax.rem(first + region + total, total)]
        start = lax.rem(base + shift - 1 + extent, extent)
        here = lax.div(start, LINE)
        values += [
            shifts_y[here, 1], shifts_y[lax.rem(here + 1, strips), 1], LINE - lax.rem(start, LINE)
        ]
    lane = lax.broadcasted_iota(jnp.int32, (1, LINE), 1)
    row = jnp.zeros((1, LINE), jnp.int32)
    for index, value in enumerate(values):
        row = jnp.where(lane == index, value, row)
    offsets[...] = row
    for axis in range(2):
        for level_pass in range(3):
            taps = cubic_weights(fractions[axis, level_pass])
            for tap, weight in enumerate(taps):
                start = 4 * (3 * axis + level_pass) + tap
                weights[start:start + 1] = jnp.full((1, LINE), weight, jnp.float32)


def taps_of(weights, axis, level_pass):
    start = 4 * (3 * axis + level_pass)
    return [weights[start + tap:start + tap + 1] for tap in range(4)]


def sweep_x_kernel(fill, offsets, weights, *refs):
    *gathered, own, own_coarse, to_near, to_far, fine_lines, coarse_lines = refs
    lines, levels, _, _ = fine_lines.shape
    rows = own.shape[3]
    slab = own_coarse.shape[2]
    starts = offsets[...]
    fine_weights = taps_of(weights, 0, 1)
    coarse_weights = taps_of(weights, 0, 2)
    fill(*gathered, fine_lines, coarse_lines)
    for line in range(lines):
        for slot in range(3):
            start = starts[0, 4 * line + slot]
            for level in range(levels):
                own[line, slot, level] = weighted(
                    fine_weights,
                    lambda tap: fine_lines[line, level, pl.ds(start + 2 - tap, rows)],
                )
        start = starts[0, 4 * line + 3]
        for level in range(levels):
            own_coarse[line, level] = weighted(
                coarse_weights,
                lambda tap: coarse_lines[line, level, pl.ds(start + 2 - tap, slab)],
            )
    near_right = lax.axis_index("gy") % 2 == 0
    half = LINE // 2
    lane = lax.broadcasted_iota(jnp.int32, (rows, LINE), 1)
    flat = lax.broadcasted_iota(jnp.int32, (slab // 2, LINE), 1)
    for level in range(levels):
        last = lines - 1
        left = jnp.where(
            lane < LINE - HALO, own[0, 1, level], pltpu.roll(own[0, 0, level], LINE - HALO, 1)
        )
        right = jnp.where(
            lane >= HALO, own[last, 1, level], pltpu.roll(own[last, 2, level], HALO, 1)
        )
        to_near[level, :rows] = jnp.where(near_right, right, left)
        to_far[level, :rows] = jnp.where(near_right, left, right)
        upper, lower = own_coarse[0, level, :slab // 2], own_coarse[0, level, slab // 2:]
        left = jnp.where(flat < half, upper, pltpu.roll(lower, half, 1))
        upper, lower = own_coarse[last, level, :slab // 2], own_coarse[last, level, slab // 2:]
        right = jnp.where(flat < half, pltpu.roll(upper, half, 1), lower)
        to_near[level, rows:] = jnp.where(near_right, right, left)
        to_far[level, rows:] = jnp.where(near_right, left, right)


def turned(weights, offset, current, left, right, lane):
    beside = jnp.where(lane < LINE // 2, right, left)

    def term(tap):
        distance = offset + 2 - tap
        outside = (lane < distance) | (lane >= LINE + distance)
        mixed = jnp.where(outside, beside, current)
        return pltpu.roll(mixed, lax.rem(LINE - distance, LINE), 1)

    return weighted(weights, term)


def sweep_y_kernel(strips, offsets, weights, own, own_coarse, from_near, from_far, out, held):
    lines, _, levels, rows, _ = own.shape
    slab = own_coarse.shape[2]
    outer_x = taps_of(weights, 0, 0)
    outer_y = taps_of(weights, 1, 0)
    inner_y = taps_of(weights, 1, 1)
    coarse_y = taps_of(weights, 1, 2)
    tall = lax.broadcasted_iota(jnp.int32, (rows, LINE), 1)
    flat = lax.broadcasted_iota(jnp.int32, (slab, LINE), 1)
    row = lax.broadcasted_iota(jnp.int32, (rows, LINE), 0)
    near_right = lax.axis_index("gy") % 2 == 0
    shifts = offsets[...]
    outer_shift, coarse_shift = shifts[0, 4 * lines], shifts[0, 4 * lines + 1]

    def received(level):
        near, far = from_near[level], from_far[level]
        left, right = jnp.where(near_right, far, near), jnp.where(near_right, near, far)
        half = LINE // 2
        return {
            "left": (left[:rows], pltpu.roll(left[:rows], LINE - HALO, 1)),
            "right": (right[:rows], pltpu.roll(right[:rows], HALO, 1)),
            "left_coarse": jnp.concatenate([pltpu.roll(left[rows:], half, 1), left[rows:]]),
            "right_coarse": jnp.concatenate([right[rows:], pltpu.roll(right[rows:], half, 1)]),
        }

    halo = [received(level) for level in range(levels)]

    def pieces(region, level):
        if region < 0:
            current = halo[level]["left"][0]
            return current, current, own[0, 0, level]
        if region == lines:
            current = halo[level]["right"][0]
            return current, own[lines - 1, 2, level], current
        left = own[region - 1, 2, level] if region else halo[level]["left"][1]
        right = own[region + 1, 0, level] if region < lines - 1 else halo[level]["right"][1]
        return own[region, 1, level], left, right

    outer = {}
    for region in range(-1, lines + 1):
        entry = 4 * lines + 2 + (3 * (region + 1) if strips > 1 else 0)
        here = shifts[0, entry]
        for level in range(levels):
            current, left, right = pieces(region, level)
            swept = turned(inner_y, here, current, left, right, tall)
            if strips > 1:
                swept = jnp.where(
                    row >= shifts[0, entry + 2],
                    turned(inner_y, shifts[0, entry + 1], current, left, right, tall),
                    swept,
                )
            held[region + 1, level] = swept
            outer[region, level] = weighted(
                outer_x, lambda tap: held[region + 1, level, 3 - tap:3 - tap + slab]
            )
    for line in range(lines):
        for level in range(levels):
            fine_field = turned(
                outer_y, outer_shift, outer[line, level],
                outer[line - 1, level], outer[line + 1, level], flat,
            )
            left = own_coarse[line - 1, level] if line else halo[level]["left_coarse"]
            right = (
                own_coarse[line + 1, level] if line < lines - 1 else halo[level]["right_coarse"]
            )
            coarse_field = turned(
                coarse_y, coarse_shift, own_coarse[line, level], left, right, flat
            )
            out[level, :, line * LINE:(line + 1) * LINE] = fine_field - coarse_field


def on_chip(count):
    return [pl.BlockSpec(memory_space=pltpu.VMEM)] * count


def scalars(count):
    return [pl.BlockSpec(memory_space=pltpu.SMEM)] * count


def local(fine_cotangent, coarse_cotangent, upstream_x, upstream_y, fractions):
    levels, slab, width = fine_cotangent.shape
    lines = width // LINE
    count_x = lax.axis_size("gx")
    count_y = lax.axis_size("gy")
    reach = count_x // 8 * slab
    rows = rounded(slab + 3)
    slabs_fine = -(-(2 * reach + 4) // slab)
    slabs_coarse = -(-(reach + 2) // slab)
    like = functools.partial(jax.ShapeDtypeStruct, dtype=fine_cotangent.dtype)
    windows = [
        pltpu.VMEM((lines, levels, (2 * slabs + 1) * slab, LINE), fine_cotangent.dtype)
        for slabs in (slabs_fine, slabs_coarse)
    ]
    limit = (4 << 20) + 12 * levels * (slabs_fine + slabs_coarse + 1) * slab * width * 4
    params = pltpu.CompilerParams(vmem_limit_bytes=limit)
    offsets, weights = pl.pallas_call(
        functools.partial(table_kernel, slab, lines, slabs_fine * slab, slabs_coarse * slab),
        out_shape=[jax.ShapeDtypeStruct((1, LINE), jnp.int32), like((4 * 6, LINE))],
        in_specs=scalars(3),
        out_specs=on_chip(2),
        compiler_params=params,
    )(upstream_x, upstream_y.T, fractions.T)
    if count_x == 8 and slab == 2 * EDGE:
        packed = jnp.concatenate([fine_cotangent, coarse_cotangent], axis=1)
        packed = lax.optimization_barrier(packed)
        edge = lax.dynamic_slice_in_dim(packed, column_side() * (slab - EDGE), EDGE, 1)
        beside = exchanged(packed, "gx", lambda i: i ^ 1)
        near = exchanged(packed, "gx", lambda i: i ^ 2)
        opposite = exchanged(edge, "gx", lambda i: i ^ 4)
        far = exchanged(packed, "gx", lambda i: i ^ 6)
        beside, near, opposite, far = lax.optimization_barrier((beside, near, opposite, far))
        relay = pl.pallas_call(
            relay_kernel,
            out_shape=like((levels, 2 * slab + EDGE, width)),
            in_specs=on_chip(3),
            out_specs=on_chip(1)[0],
            compiler_params=params,
        )(near, far, opposite)
        relay = exchanged(relay, "gx", lambda i: i ^ 1)
        fill = fill_pieces
        gathered = packed, beside, near, far, relay
    else:
        fill = fill_whole
        gathered = ring_window(fine_cotangent, slabs_fine), ring_window(coarse_cotangent, slabs_coarse)
    sent = like((levels, rows + slab // 2, LINE))
    own, own_coarse, to_near, to_far = pl.pallas_call(
        functools.partial(sweep_x_kernel, fill),
        out_shape=[
            like((lines, 3, levels, rows, LINE)), like((lines, levels, slab, LINE)), sent, sent,
        ],
        in_specs=on_chip(2 + len(gathered)),
        out_specs=on_chip(4),
        scratch_shapes=windows,
        compiler_params=params,
    )(offsets, weights, *gathered)
    from_near = exchanged(to_near, "gy", lambda j: j ^ 1)
    from_far = exchanged(to_far, "gy", lambda j: (j - 1 + 2 * (j % 2)) % count_y)
    return pl.pallas_call(
        functools.partial(sweep_y_kernel, upstream_y.shape[1]),
        out_shape=like((levels, slab, width)),
        in_specs=on_chip(6),
        out_specs=on_chip(1)[0],
        scratch_shapes=[pltpu.VMEM((lines + 2, levels, rows, LINE), fine_cotangent.dtype)],
        compiler_params=params,
    )(offsets, weights, own, own_coarse, from_near, from_far)


def solution(mesh):
    placed = (P(None, "gx", "gy"), P(None, "gx", "gy"), P(), P(), P())

    def step(*args):
        return local(*args)

    step = jax.shard_map(
        step, mesh=mesh, in_specs=placed, out_specs=P(None, "gx", "gy"), check_vma=False
    )
    return step
```

```python
import functools

import jax
import jax.numpy as jnp
from jax import lax
from jax.experimental import pallas as pl
from jax.experimental.pallas import tpu as pltpu
from jax.sharding import PartitionSpec as P


LINE = 128
MAXDY = 32
EDGE = 8
HALO = MAXDY + 2


def rounded(rows):
    return -(-rows // EDGE) * EDGE


def exchanged(block, axis, partner):
    return lax.ppermute(block, axis, [(i, partner(i)) for i in range(lax.axis_size(axis))])


def shifted(block, axis, distance):
    count = lax.axis_size(axis)
    return exchanged(block, axis, lambda i: (i + distance) % count)


def ring_window(block, slabs):
    lower = [shifted(block, "gx", distance) for distance in range(slabs, 0, -1)]
    upper = [shifted(block, "gx", -distance) for distance in range(1, slabs + 1)]
    return jnp.concatenate(lower + [block] + upper, axis=1)


def cubic_weights(fraction):
    position = 1.0 - fraction
    return (
        -position * (position - 1.0) * (position - 2.0) * (1.0 / 6.0),
        (position + 1.0) * (position - 1.0) * (position - 2.0) * 0.5,
        -(position + 1.0) * position * (position - 2.0) * 0.5,
        (position + 1.0) * position * (position - 1.0) * (1.0 / 6.0),
    )


def weighted(weights, term):
    summed = weights[0] * term(0)
    for tap in range(1, len(weights)):
        summed = summed + weights[tap] * term(tap)
    return summed


def aligned(start, size):
    return pl.ds(pl.multiple_of(start, EDGE), size)


def column_side():
    return lax.axis_index("gx") % 2


def layer_side():
    return lax.axis_index("gx") // 2 % 2


def relay_kernel(near, far, opposite, relay):
    levels, both, width = near.shape
    slab = both // 2
    column = column_side()
    start = (1 - column) * (slab - EDGE)
    swapped = (column + layer_side()) % 2
    row = lax.broadcasted_iota(jnp.int32, (levels, EDGE, width), 1)
    low = (row < EDGE // 2) == (column == 1)

    def send(whole, partial):
        relay[:, :both] = whole[...]
        relay[:, both:] = jnp.where(low, partial[:, aligned(start, EDGE)], opposite[...])

    @pl.when(swapped == 0)
    def _():
        send(near, far)

    @pl.when(swapped == 1)
    def _():
        send(far, near)


def fill_whole(fine, coarse, fine_lines, coarse_lines):
    for line in range(fine_lines.shape[0]):
        lanes = slice(line * LINE, (line + 1) * LINE)
        fine_lines[line] = fine[:, :, lanes]
        coarse_lines[line] = coarse[:, :, lanes]


def fill_pieces(own, beside, near, far, relay, fine_lines, coarse_lines):
    both = own.shape[1]
    slab = both // 2
    column = 1 - 2 * column_side()
    layer = 1 - 2 * layer_side()
    fine_center = (fine_lines.shape[2] - slab) // 2
    coarse_center = (coarse_lines.shape[2] - slab) // 2
    below = fine_center - 2 * slab - EDGE
    above = fine_center + 3 * slab
    for line in range(fine_lines.shape[0]):
        lanes = slice(line * LINE, (line + 1) * LINE)
        for piece, slabs in (
            (own, 0), (beside, column), (near, 2 * layer), (far, -2 * layer), (relay, -column),
        ):
            fine_lines[line, :, aligned(fine_center + slabs * slab, slab)] = piece[:, :slab, lanes]
            coarse_lines[line, :, aligned(coarse_center + slabs * slab, slab)] = (
                piece[:, slab:both, lanes]
            )
        for row in (below, above):
            fine_lines[line, :, row:row + EDGE] = relay[:, both:, lanes]


def table_kernel(slab, lines, fine_center, coarse_center,
                 shifts_x, shifts_y, fractions, offsets, weights):
    total = shifts_x.shape[1]
    strips = shifts_y.shape[0]
    first = lax.axis_index("gy") * lines
    base = lax.axis_index("gx") * slab
    extent = lax.axis_size("gx") * slab
    values = []
    for line in range(lines):
        inner = shifts_x[1, first + line]
        for slot in range(3):
            region = lax.rem(first + line + slot - 1 + total, total)
            values.append(fine_center - 1 + inner + shifts_x[0, region])
        values.append(coarse_center + shifts_x[2, first + line])
    strip = lax.div(base, LINE)
    values += [shifts_y[strip, 0], shifts_y[strip, 2]]
    for region in range(-1, lines + 1):
        shift = shifts_x[0, lax.rem(first + region + total, total)]
        start = lax.rem(base + shift - 1 + extent, extent)
        here = lax.div(start, LINE)
        values += [
            shifts_y[here, 1], shifts_y[lax.rem(here + 1, strips), 1], LINE - lax.rem(start, LINE)
        ]
    lane = lax.broadcasted_iota(jnp.int32, (1, LINE), 1)
    row = jnp.zeros((1, LINE), jnp.int32)
    for index, value in enumerate(values):
        row = jnp.where(lane == index, value, row)
    offsets[...] = row
    for axis in range(2):
        for level_pass in range(3):
            taps = cubic_weights(fractions[axis, level_pass])
            for tap, weight in enumerate(taps):
                start = 4 * (3 * axis + level_pass) + tap
                weights[start:start + 1] = jnp.full((1, LINE), weight, jnp.float32)
    outer, inner = (cubic_weights(fractions[0, level_pass]) for level_pass in range(2))
    for tap in range(7):
        products = [outer[i] * inner[tap - i] for i in range(4) if 0 <= tap - i < 4]
        weight = functools.reduce(lambda total, product: total + product, products)
        weights[24 + tap:25 + tap] = jnp.full((1, LINE), weight, jnp.float32)


def taps_of(weights, axis, level_pass):
    start = 4 * (3 * axis + level_pass)
    return [weights[start + tap:start + tap + 1] for tap in range(4)]


def sweep_x_kernel(fill, offsets, weights, *refs):
    *gathered, own, own_coarse, to_near, to_far, fine_lines, coarse_lines = refs
    lines, levels, _, _ = fine_lines.shape
    rows = own.shape[3]
    slab = own_coarse.shape[2]
    starts = offsets[...]
    if rows == slab:
        reach_up, fine_weights = 5, [weights[24 + tap:25 + tap] for tap in range(7)]
    else:
        reach_up, fine_weights = 2, taps_of(weights, 0, 1)
    coarse_weights = taps_of(weights, 0, 2)
    fill(*gathered, fine_lines, coarse_lines)
    for line in range(lines):
        for slot in range(3):
            start = starts[0, 4 * line + slot]
            for level in range(levels):
                own[line, slot, level] = weighted(
                    fine_weights,
                    lambda tap: fine_lines[line, level, pl.ds(start + reach_up - tap, rows)],
                )
        start = starts[0, 4 * line + 3]
        for level in range(levels):
            own_coarse[line, level] = weighted(
                coarse_weights,
                lambda tap: coarse_lines[line, level, pl.ds(start + 2 - tap, slab)],
            )
    near_right = lax.axis_index("gy") % 2 == 0
    half = LINE // 2
    lane = lax.broadcasted_iota(jnp.int32, (rows, LINE), 1)
    flat = lax.broadcasted_iota(jnp.int32, (slab // 2, LINE), 1)
    for level in range(levels):
        last = lines - 1
        left = jnp.where(
            lane < LINE - HALO, own[0, 1, level], pltpu.roll(own[0, 0, level], LINE - HALO, 1)
        )
        right = jnp.where(
            lane >= HALO, own[last, 1, level], pltpu.roll(own[last, 2, level], HALO, 1)
        )
        to_near[level, :rows] = jnp.where(near_right, right, left)
        to_far[level, :rows] = jnp.where(near_right, left, right)
        upper, lower = own_coarse[0, level, :slab // 2], own_coarse[0, level, slab // 2:]
        left = jnp.where(flat < half, upper, pltpu.roll(lower, half, 1))
        upper, lower = own_coarse[last, level, :slab // 2], own_coarse[last, level, slab // 2:]
        right = jnp.where(flat < half, pltpu.roll(upper, half, 1), lower)
        to_near[level, rows:] = jnp.where(near_right, right, left)
        to_far[level, rows:] = jnp.where(near_right, left, right)


def turned(weights, offset, current, left, right, lane):
    beside = jnp.where(lane < LINE // 2, right, left)

    def term(tap):
        distance = offset + 2 - tap
        outside = (lane < distance) | (lane >= LINE + distance)
        mixed = jnp.where(outside, beside, current)
        return pltpu.roll(mixed, lax.rem(LINE - distance, LINE), 1)

    return weighted(weights, term)


def turned_ends(weights, offset, low, high, low_left, high_right, lane):
    beside = jnp.where(lane < LINE // 2, high_right, low_left)

    def term(tap):
        distance = offset + 2 - tap
        outside = (lane < distance) | (lane >= LINE + distance)
        centre = jnp.where(lane < LINE // 2 + distance, low, high)
        mixed = jnp.where(outside, beside, centre)
        return pltpu.roll(mixed, lax.rem(LINE - distance, LINE), 1)

    return weighted(weights, term)


def sweep_y_kernel(offsets, weights, own, own_coarse, from_near, from_far, out,
                   held, result, finished):
    lines, _, levels, rows, _ = own.shape
    slab = own_coarse.shape[2]
    outer_x = taps_of(weights, 0, 0)
    outer_y = taps_of(weights, 1, 0)
    inner_y = taps_of(weights, 1, 1)
    coarse_y = taps_of(weights, 1, 2)
    tall = lax.broadcasted_iota(jnp.int32, (rows, LINE), 1)
    flat = lax.broadcasted_iota(jnp.int32, (slab, LINE), 1)
    row = lax.broadcasted_iota(jnp.int32, (rows, LINE), 0)
    near_right = lax.axis_index("gy") % 2 == 0
    shifts = offsets[...]
    outer_shift, coarse_shift = shifts[0, 4 * lines], shifts[0, 4 * lines + 1]

    def received(level):
        near, far = from_near[level], from_far[level]
        left, right = jnp.where(near_right, far, near), jnp.where(near_right, near, far)
        half = LINE // 2
        return {
            "left": (left[:rows], pltpu.roll(left[:rows], LINE - HALO, 1)),
            "right": (right[:rows], pltpu.roll(right[:rows], HALO, 1)),
            "left_coarse": jnp.concatenate([pltpu.roll(left[rows:], half, 1), left[rows:]]),
            "right_coarse": jnp.concatenate([right[rows:], pltpu.roll(right[rows:], half, 1)]),
        }

    halo = [received(level) for level in range(levels)]

    def pieces(region, level):
        if region < 0:
            current = halo[level]["left"][0]
            return current, current, own[0, 0, level]
        if region == lines:
            current = halo[level]["right"][0]
            return current, own[lines - 1, 2, level], current
        left = own[region - 1, 2, level] if region else halo[level]["left"][1]
        right = own[region + 1, 0, level] if region < lines - 1 else halo[level]["right"][1]
        return own[region, 1, level], left, right

    outer = {}
    if rows == slab:
        here = shifts[0, 4 * lines + 2]
        for level in range(levels):
            for region in range(lines):
                outer[region, level] = turned(inner_y, here, *pieces(region, level), flat)
            outer[-1, level] = outer[lines, level] = turned_ends(
                inner_y, here, halo[level]["right"][0], halo[level]["left"][0],
                own[lines - 1, 2, level], own[0, 0, level], flat,
            )
    else:
        for region in range(-1, lines + 1):
            entry = 4 * lines + 2 + 3 * (region + 1)
            for level in range(levels):
                current, left, right = pieces(region, level)
                held[region + 1, level] = jnp.where(
                    row >= shifts[0, entry + 2],
                    turned(inner_y, shifts[0, entry + 1], current, left, right, tall),
                    turned(inner_y, shifts[0, entry], current, left, right, tall),
                )
                outer[region, level] = weighted(
                    outer_x, lambda tap: held[region + 1, level, 3 - tap:3 - tap + slab]
                )
    copies = []
    for level in range(levels):
        for line in range(lines):
            fine_field = turned(
                outer_y, outer_shift, outer[line, level],
                outer[line - 1, level], outer[line + 1, level], flat,
            )
            left = own_coarse[line - 1, level] if line else halo[level]["left_coarse"]
            right = (
                own_coarse[line + 1, level] if line < lines - 1 else halo[level]["right_coarse"]
            )
            coarse_field = turned(
                coarse_y, coarse_shift, own_coarse[line, level], left, right, flat
            )
            result[level, :, line * LINE:(line + 1) * LINE] = fine_field - coarse_field
        copies.append(
            pltpu.make_async_copy(result.at[level], out.at[level], finished.at[level])
        )
        copies[-1].start()
    for copy in copies:
        copy.wait()


def on_chip(count):
    return [pl.BlockSpec(memory_space=pltpu.VMEM)] * count


def scalars(count):
    return [pl.BlockSpec(memory_space=pltpu.SMEM)] * count


def local(fine_cotangent, coarse_cotangent, upstream_x, upstream_y, fractions):
    levels, slab, width = fine_cotangent.shape
    lines = width // LINE
    count_x = lax.axis_size("gx")
    count_y = lax.axis_size("gy")
    reach = count_x // 8 * slab
    rows = slab if upstream_y.shape[1] == 1 else rounded(slab + 3)
    slabs_fine = -(-(2 * reach + 4) // slab)
    slabs_coarse = -(-(reach + 2) // slab)
    like = functools.partial(jax.ShapeDtypeStruct, dtype=fine_cotangent.dtype)
    windows = [
        pltpu.VMEM((lines, levels, (2 * slabs + 1) * slab, LINE), fine_cotangent.dtype)
        for slabs in (slabs_fine, slabs_coarse)
    ]
    limit = (4 << 20) + 12 * levels * (slabs_fine + slabs_coarse + 1) * slab * width * 4
    params = pltpu.CompilerParams(vmem_limit_bytes=limit)
    offsets, weights = pl.pallas_call(
        functools.partial(table_kernel, slab, lines, slabs_fine * slab, slabs_coarse * slab),
        out_shape=[jax.ShapeDtypeStruct((1, LINE), jnp.int32), like((32, LINE))],
        in_specs=scalars(3),
        out_specs=on_chip(2),
        compiler_params=params,
    )(upstream_x, upstream_y.T, fractions.T)
    if count_x == 8 and slab == 2 * EDGE:
        packed = jnp.concatenate([fine_cotangent, coarse_cotangent], axis=1)
        packed = lax.optimization_barrier(packed)
        edge = lax.dynamic_slice_in_dim(packed, column_side() * (slab - EDGE), EDGE, 1)
        beside = exchanged(packed, "gx", lambda i: i ^ 1)
        near = exchanged(packed, "gx", lambda i: i ^ 2)
        opposite = exchanged(edge, "gx", lambda i: i ^ 4)
        far = exchanged(packed, "gx", lambda i: i ^ 6)
        relay = pl.pallas_call(
            relay_kernel,
            out_shape=like((levels, 2 * slab + EDGE, width)),
            in_specs=on_chip(3),
            out_specs=on_chip(1)[0],
            compiler_params=params,
        )(near, far, opposite)
        relay = exchanged(relay, "gx", lambda i: i ^ 1)
        fill = fill_pieces
        gathered = packed, beside, near, far, relay
    else:
        fill = fill_whole
        gathered = ring_window(fine_cotangent, slabs_fine), ring_window(coarse_cotangent, slabs_coarse)
    sent = like((levels, rows + slab // 2, LINE))
    own, own_coarse, to_near, to_far = pl.pallas_call(
        functools.partial(sweep_x_kernel, fill),
        out_shape=[
            like((lines, 3, levels, rows, LINE)), like((lines, levels, slab, LINE)), sent, sent,
        ],
        in_specs=on_chip(2 + len(gathered)),
        out_specs=on_chip(4),
        scratch_shapes=windows,
        compiler_params=params,
    )(offsets, weights, *gathered)
    from_near = exchanged(to_near, "gy", lambda j: j ^ 1)
    from_far = exchanged(to_far, "gy", lambda j: (j - 1 + 2 * (j % 2)) % count_y)
    return pl.pallas_call(
        sweep_y_kernel,
        out_shape=like((levels, slab, width)),
        in_specs=on_chip(6),
        out_specs=pl.BlockSpec(memory_space=pl.ANY),
        scratch_shapes=[
            pltpu.VMEM((lines + 2, levels, rows, LINE), fine_cotangent.dtype),
            pltpu.VMEM((levels, slab, width), fine_cotangent.dtype),
            pltpu.SemaphoreType.DMA((levels,)),
        ],
        compiler_params=params,
    )(offsets, weights, own, own_coarse, from_near, from_far)


def solution(mesh):
    placed = (P(None, "gx", "gy"), P(None, "gx", "gy"), P(), P(), P())

    def step(*args):
        return local(*args)

    step = jax.shard_map(
        step, mesh=mesh, in_specs=placed, out_specs=P(None, "gx", "gy"), check_vma=False
    )
    return step
```
